32 devices in a mesh: clus: 16 (over z, y, x), sub: 2 (over core).
Axes of the slice: x: 2, y: 2, z: 4, core: 2. Of those that a mesh axis runs over, the one named last changes fastest.
Arguments:
- dual_ops: float32 [64, 1536, 1536], P(('clus', 'sub')), may hold values from 0 to 3, as said below
- rigid_modes: float32 [64, 6, 1536], P(('clus', 'sub')), may hold values from -6 to 6
- members: int32 [64, 4, 1536], P(('clus', 'sub')), may hold values from 0 to 6144, as said below
- coarse_inverse: float32 [384, 384], P(('clus', 'sub')), may hold values from -1 to 1
- dual_rhs: float32 [64, 1536, 128], P(('clus', 'sub')), may hold values from -12 to 12
- coarse_rhs: float32 [64, 6, 128], P(('clus', 'sub')), may hold values from -512 to 512
Outputs:
- multipliers: float32 [64, 1536, 128], P(('clus', 'sub'))
- projected: float32 [64, 1536, 128], P(('clus', 'sub'))
The draws below stay inside these ranges and needn't reach their ends.
Inputs may be any that keep to these rules, and one draw needn't show every extreme that they name: Every slot's group lists the slot itself first (its own position (s % 2) * 1536 + i), holds 1 to 4 slots of different subdomains, and is the same set for every slot in it; the group of every slot i >= 256 is that slot and one slot >= 256 of the other subdomain of the same device (members[s, 2:, i] = EMPTY); exported entries name only slots among the first 256 of a subdomain on devices with o in 0, 1, 2 that exist. Number the exported slots of a device k = 256 j + i for slot i of its j-th subdomain, and let E = 512: those with k < E / 4 are named only by groups of the other device of the same cluster; E / 4 <= k < E / 2 only by the device of cluster c + 1 with the same t; E / 2 <= k < 3 E / 4 only by the device of cluster c - 1 with the same t; 3 E / 4 <= k < 7 E / 8 only by the other device of the same cluster and the devices of cluster c + 1; 7 E / 8 <= k only by the other device of the same cluster and the devices of cluster c - 1. In each dual_ops[s] every row's off-diagonal entries sum in magnitude to less than its diagonal entry.
All inputs are finite; a program needn't handle non-finite values.
Results may differ from the reference program's by a relative error of at most 0.00015.
Values sent between devices are 32-bit elements; how exact they have to be, the bound alone decides.
A program may use at most 128 MiB of HBM per device.

```python
import math
import jax
import jax.numpy as jnp
from jax import lax

M = 1536
ESUB = 256
K = 4
NRB = 6
SUB_DEV = 2
NRHS = 128
ITERS = 2
SUBS = 64
NC = 384
N_CLUS = 16
N_SUB = 2


def perm_rows(key, count, length):
    streams = jax.random.split(key, count)
    return jax.vmap(lambda single: jax.random.permutation(single, length))(streams).astype(jnp.int32)


def inverse_rows(table):
    return jnp.argsort(table, axis=-1).astype(jnp.int32)


def take_rows(table, index):
    return jnp.take_along_axis(table, index, axis=1)


def draw_members(key, part):
    export_rows = SUB_DEV * ESUB
    quarter = export_rows // 4
    eighth = export_rows // 8
    local_rows = SUB_DEV * M
    pad_index = local_rows + 6 * export_rows
    inner_slots = M - ESUB
    devices = N_CLUS * N_SUB
    streams = jax.random.split(jax.random.fold_in(key, 7), 4)
    side_order = perm_rows(streams[0], N_CLUS, quarter)
    side_back = inverse_rows(side_order)
    face_order = perm_rows(streams[1], N_CLUS, quarter)
    face_back = inverse_rows(face_order)
    corner = perm_rows(streams[2], 4 * N_CLUS, eighth).reshape(N_CLUS, 4, eighth)
    corner_back = inverse_rows(corner)
    pair_order = perm_rows(streams[3], devices * (SUB_DEV // 2), inner_slots).reshape(devices, SUB_DEV // 2, inner_slots)
    pair_back = inverse_rows(pair_order)
    device = jnp.arange(devices, dtype=jnp.int32)
    cluster = device // N_SUB
    half_index = device % N_SUB
    other_half = 1 - half_index
    lower_cluster = jnp.maximum(cluster - 1, 0)
    has_upper = (cluster < N_CLUS - 1)[:, None]
    has_lower = (cluster > 0)[:, None]
    up_start = 3 * quarter
    down_start = 3 * quarter + eighth

    def base(offset, which):
        value = local_rows + (2 * offset + which) * export_rows + jnp.zeros_like(device)
        return value.astype(jnp.int32)[:, None]

    def own_slots(first, count):
        position = first + jnp.arange(count, dtype=jnp.int32)
        return jnp.broadcast_to((position // ESUB * M + position % ESUB)[None, :], (devices, count))

    def padded(count):
        return jnp.full((devices, count), pad_index, jnp.int32)
    side_partner = jnp.where(half_index[:, None] == 0, side_order[cluster], side_back[cluster])
    part_side = jnp.stack([own_slots(0, quarter), base(1, other_half) + side_partner, padded(quarter), padded(quarter)], -1)
    upper_face = jnp.where(has_upper, base(2, half_index) + 2 * quarter + face_order[cluster], pad_index)
    part_up = jnp.stack([own_slots(quarter, quarter), upper_face, padded(quarter), padded(quarter)], -1)
    lower_face = jnp.where(has_lower, base(0, half_index) + quarter + face_back[lower_cluster], pad_index)
    part_down = jnp.stack([own_slots(2 * quarter, quarter), lower_face, padded(quarter), padded(quarter)], -1)
    group_up = corner_back[cluster, half_index]
    corner_up = jnp.stack([own_slots(up_start, eighth), base(1, other_half) + up_start + take_rows(corner[cluster, other_half], group_up), jnp.where(has_upper, base(2, 0) + down_start + take_rows(corner[cluster, 2], group_up), pad_index), jnp.where(has_upper, base(2, 1) + down_start + take_rows(corner[cluster, 3], group_up), pad_index)], -1)
    group_down = corner_back[lower_cluster, 2 + half_index]
    corner_down = jnp.stack([own_slots(down_start, eighth), jnp.where(has_lower, base(1, other_half) + down_start + take_rows(corner[lower_cluster, 3 - half_index], group_down), pad_index), jnp.where(has_lower, base(0, 0) + up_start + take_rows(corner[lower_cluster, 0], group_down), pad_index), jnp.where(has_lower, base(0, 1) + up_start + take_rows(corner[lower_cluster, 1], group_down), pad_index)], -1)
    exported = jnp.concatenate([part_side, part_up, part_down, corner_up, corner_down], axis=1)
    exported = exported.reshape(devices, SUB_DEV, ESUB, 4)
    subdomain = jnp.arange(SUB_DEV, dtype=jnp.int32)
    even_sub = (subdomain % 2 == 0)[None, :, None]
    partner_slot = jnp.where(even_sub, pair_order[:, subdomain // 2, :], pair_back[:, subdomain // 2, :])
    partner_sub = jnp.where(subdomain % 2 == 0, subdomain + 1, subdomain - 1)[None, :, None]
    slot_index = jnp.arange(inner_slots, dtype=jnp.int32)[None, None, :]
    own_inner = jnp.broadcast_to(subdomain[None, :, None] * M + ESUB + slot_index, (devices, SUB_DEV, inner_slots))
    partner_inner = partner_sub * M + ESUB + partner_slot
    fill_inner = jnp.full((devices, SUB_DEV, inner_slots), pad_index, jnp.int32)
    internal = jnp.stack([own_inner, partner_inner, fill_inner, fill_inner], -1)
    whole = jnp.concatenate([exported, internal], axis=2).reshape(SUBS, M, 4)
    return jnp.transpose(whole, (0, 2, 1)).astype(jnp.int32)


def draw_dual_ops(key, part):
    streams = jax.random.split(jax.random.fold_in(key, 3), 2)
    position = jnp.arange(M, dtype=jnp.float32)
    distance = jnp.abs(position[:, None] - position[None, :])
    level = 0.8 / (1.5 * 512.0 * math.log(1.0 + M / 512.0))
    envelope = level / (1.0 + distance / 256.0)
    on_diagonal = distance == 0.0

    def one_operator(index):
        diagonal = jax.random.uniform(jax.random.fold_in(streams[0], index), (M, 1), jnp.float32, 1.0, 3.0)
        rough = jax.random.uniform(jax.random.fold_in(streams[1], index), (M, M), jnp.float32, -1.0, 1.0)
        return jnp.where(on_diagonal, diagonal, envelope * (1.0 + 0.5 * rough))
    return lax.map(one_operator, jnp.arange(SUBS, dtype=jnp.int32))


def draw_coarse_inverse(key, part):
    streams = jax.random.split(jax.random.fold_in(key, 5), 2)
    diagonal = jax.random.uniform(streams[0], (NC, 1), jnp.float32, 1.0, 2.0)
    spread = jax.random.uniform(streams[1], (NC, NC), jnp.float32, -1.0, 1.0) * math.sqrt(3.0)
    spread = spread * (0.5 / math.sqrt(NC))
    index = jnp.arange(NC, dtype=jnp.int32)
    identity = (index[:, None] == index[None, :]).astype(jnp.float32)
    return 2.0 / M * (identity * diagonal + (1.0 - identity) * spread)


def draw_dual_rhs(key, part):
    stream = jax.random.fold_in(key, 9)
    ramp = (jnp.arange(SUBS, dtype=jnp.float32) / max(SUBS - 1, 1))[:, None, None]
    values = jax.random.truncated_normal(stream, -4.0, 4.0, (SUBS, M, NRHS), jnp.float32)
    return values * (1.0 + 2.0 * ramp)


def block_scale(stream_key, extent, pieces, smallest, high):
    loudness = 1.0
    for dim, blocks in pieces:
        heights = jax.random.uniform(jax.random.fold_in(jax.random.fold_in(stream_key, 6), dim), (blocks,), jnp.float32, smallest / len(pieces), high / len(pieces))
        loudness = loudness * jnp.repeat(jnp.exp(heights), extent[dim] // blocks).reshape((-1,) + (1,) * (len(extent) - 1 - dim))
    return loudness


def normal_values(key, extent, deviation, most, pieces=(), kind=jnp.bfloat16):
    array = jax.random.normal(key, extent, jnp.float32) * deviation
    if len(pieces) > 0:
        array = block_scale(key, extent, pieces, -0.22, 0.18) * array
    return jnp.clip(array, min=-most, max=most).astype(kind)


def setup_inputs(seed: int = 0) -> dict:
    seeds = jax.random.split(jax.random.key(seed), 7)
    dual_ops = draw_dual_ops(jax.random.fold_in(seeds[6], 71), 0)
    rigid_modes = normal_values(seeds[1], (SUBS, NRB, M), 1.0, 6.0, ((0, 32),), jnp.float32)
    members = draw_members(jax.random.fold_in(seeds[6], 71), 0)
    coarse_inverse = draw_coarse_inverse(jax.random.fold_in(seeds[6], 71), 0)
    dual_rhs = draw_dual_rhs(jax.random.fold_in(seeds[6], 71), 0)
    coarse_rhs = normal_values(seeds[5], (SUBS, NRB, NRHS), (M // 16), 512.0, ((0, 32),), jnp.float32)
    return dict(dual_ops=dual_ops, rigid_modes=rigid_modes, members=members, coarse_inverse=coarse_inverse, dual_rhs=dual_rhs, coarse_rhs=coarse_rhs)


def reference(dual_ops, rigid_modes, members, coarse_inverse, dual_rhs, coarse_rhs):
    devices = N_CLUS * N_SUB
    local_rows = SUB_DEV * M
    export_rows = SUB_DEV * ESUB
    pad_index = local_rows + 6 * export_rows
    slots_all = SUBS * M
    tables = jnp.transpose(members.reshape(devices, SUB_DEV, K, M), (2, 0, 1, 3)).reshape(K, devices, local_rows)
    device = jnp.arange(devices, dtype=jnp.int32)[None, :, None]
    offset = tables - local_rows
    cycle_block = offset // export_rows
    within = offset % export_rows
    target = (device // N_SUB + cycle_block // 2 - 1) * N_SUB + cycle_block % 2
    remote = target * local_rows + (within // ESUB) * M + within % ESUB
    global_slot = jnp.where(tables < local_rows, device * local_rows + tables,
                            jnp.where(tables >= pad_index, slots_all, remote))
    global_slot = global_slot.reshape(K, slots_all).astype(jnp.int32)
    group_size = jnp.sum((global_slot < slots_all).astype(jnp.float32), axis=0)[:, None]
    empty_row = jnp.zeros((1, NRHS), jnp.float32)

    def jump_part(field):
        flat_field = field.reshape(slots_all, NRHS)
        pool_rows = jnp.concatenate([flat_field, empty_row], axis=0)
        group_total = jnp.take(pool_rows, global_slot[0], axis=0)
        for member in range(1, K):
            group_total = group_total + jnp.take(pool_rows, global_slot[member], axis=0)
        return (flat_field - group_total / group_size).reshape(field.shape)

    def blockwise(field):
        return jnp.einsum("smq,sqn->smn", dual_ops, field, precision=lax.Precision.HIGHEST)

    def lift(coarse):
        weights = jnp.dot(coarse_inverse, coarse, precision=lax.Precision.HIGHEST, preferred_element_type=jnp.float32)
        weights = weights.reshape(SUBS, NRB, NRHS)
        return jump_part(jnp.einsum("skm,skn->smn", rigid_modes, weights, precision=lax.Precision.HIGHEST))

    def restrict(field):
        return jnp.einsum("skm,smn->skn", rigid_modes, field, precision=lax.Precision.HIGHEST).reshape(NC, NRHS)

    def project(field):
        return field - lift(restrict(field))

    multipliers = lift(coarse_rhs.reshape(NC, NRHS))
    residual_now = jump_part(dual_rhs - blockwise(multipliers))
    projected = project(residual_now)
    direction = projected
    norm_now = jnp.sum(projected * projected, axis=(0, 1))
    for iteration in range(ITERS):
        along = jump_part(blockwise(direction))
        step_size = norm_now / jnp.sum(direction * along, axis=(0, 1))
        multipliers = multipliers + step_size[None, None, :] * direction
        residual_now = residual_now - step_size[None, None, :] * along
        projected = project(residual_now)
        if iteration + 1 < ITERS:
            norm_next = jnp.sum(projected * projected, axis=(0, 1))
            direction = projected + (norm_next / norm_now)[None, None, :] * direction
            norm_now = norm_next
    return multipliers, projected
```

```python
import functools
import jax
import jax.numpy as jnp
from jax import lax
from jax.experimental import pallas as pl
from jax.experimental.pallas import tpu as pltpu
from jax.sharding import PartitionSpec as P

ESUB = 256
LANES = 128
TILE = 256
BIG = 512
POOL = 768
ROUNDS = 4
MESH = pl.DeviceIdType.MESH
F32 = jnp.float32
BF16 = jnp.bfloat16


def split(value):
    high = value.astype(BF16)
    low = (value - high.astype(F32)).astype(BF16)
    return jnp.concatenate([high, low], axis=1)


def mm(left, right):
    return jnp.dot(left, right, preferred_element_type=F32)


def fold(wide):
    return wide[:, :LANES] + wide[:, LANES:]


def kernel(
    ops_hbm, modes_field, modes, inner0, inner1, outer, cinv, rhs, crhs,
    mult, proj,
    ops_hi, ops_lo, ops_buf, perm0, perm1, share, lift_cat, image_cat, cat,
    field, jumped, image, past, pool, coarse, near,
    ops_sem, halo_send, halo_recv, near_send, near_recv, ag_send, ag_recv, fwd_send, fwd_recv,
    *, clusters,
):
    c = lax.axis_index("clus")
    t = lax.axis_index("sub")
    other = 1 - t
    has_up = c < clusters - 1
    has_down = c > 0
    up = jnp.minimum(c + 1, clusters - 1)
    down = jnp.maximum(c - 1, 0)
    slot = (c % 4) * 2 + t
    half = ops_hi.shape[0] // 2
    tiles = 2 * ops_hi.shape[0]
    per = tiles // 2
    rows = per * TILE
    inner = rows - ESUB

    def load(chunk, buf):
        return pltpu.make_async_copy(ops_hbm.at[chunk], ops_buf.at[buf], ops_sem.at[buf])

    load(0, 0).start()
    load(1, 1).start()

    near[...] = jnp.zeros_like(near)
    barrier = pltpu.get_barrier_semaphore()

    @pl.loop(1, clusters)
    def _(k):
        pl.semaphore_signal(barrier, inc=1, device_id=((c + k) % clusters, t), device_id_type=MESH)

    pl.semaphore_signal(barrier, inc=1, device_id=(c, other), device_id_type=MESH)

    @pl.when(has_up)
    def _():
        pl.semaphore_signal(barrier, inc=1, device_id=(up, other), device_id_type=MESH)

    @pl.when(has_down)
    def _():
        pl.semaphore_signal(barrier, inc=1, device_id=(down, other), device_id_type=MESH)

    @pl.when(c == 0)
    def _():
        for r in range(ROUNDS):
            pool[r, 256:448, :] = jnp.zeros((192, LANES), F32)
            pool[r, 640:704, :] = jnp.zeros((64, LANES), F32)

    @pl.when(c == clusters - 1)
    def _():
        for r in range(ROUNDS):
            pool[r, 448:640, :] = jnp.zeros((192, LANES), F32)
            pool[r, 704:768, :] = jnp.zeros((64, LANES), F32)

    coarse[0, t, c] = crhs[...]
    near[slot] = cinv[...]

    @pl.when(has_up & has_down)
    def _():
        pl.semaphore_wait(barrier, clusters + 2)

    @pl.when(jnp.logical_not(has_up & has_down))
    def _():
        pl.semaphore_wait(barrier, clusters + 1)

    def halo_copies(source, r):
        top, low = source.at[0], source.at[per]
        plan = [
            (top, 0, 128, 0, (c, other)),
            (low, 128, 128, 128, (c, other)),
            (top, 128, 128, 256, (up, t)),
            (low, 128, 64, 384, (up, t)),
            (low, 128, 64, 640, (up, other)),
            (low, 0, 128, 448, (down, t)),
            (low, 192, 64, 576, (down, t)),
            (low, 192, 64, 704, (down, other)),
        ]
        copies = [
            pltpu.make_async_remote_copy(
                src_ref=ref.at[pl.ds(start, size)],
                dst_ref=pool.at[r, pl.ds(to, size)],
                send_sem=halo_send.at[r, n],
                recv_sem=halo_recv.at[r, n],
                device_id=device,
                device_id_type=MESH,
            )
            for n, (ref, start, size, to, device) in enumerate(plan)
        ]
        return copies[:2], copies[2:5], copies[5:]

    def near_copies():
        return [
            pltpu.make_async_remote_copy(
                src_ref=cinv,
                dst_ref=near.at[slot],
                send_sem=near_send.at[n],
                recv_sem=near_recv.at[n],
                device_id=device,
                device_id_type=MESH,
            )
            for n, device in enumerate([(c, other), (up, t), (up, other), (down, t), (down, other)])
        ]

    def start_all(groups):
        both, ups, downs = groups

        @pl.when(has_up)
        def _():
            for copy in ups:
                copy.start()

        @pl.when(has_down)
        def _():
            for copy in downs:
                copy.start()

        for copy in both:
            copy.start()

    def wait_all(groups):
        both, ups, downs = groups
        for copy in both:
            copy.wait_recv()
            copy.wait_send()

        @pl.when(has_up)
        def _():
            for copy in ups:
                copy.wait_send()
            for copy in downs:
                copy.wait_recv()

        @pl.when(has_down)
        def _():
            for copy in downs:
                copy.wait_send()
            for copy in ups:
                copy.wait_recv()

    def near_groups():
        copies = near_copies()
        return copies[:1], copies[1:3], copies[3:]

    def ag_copy(r, k):
        return pltpu.make_async_remote_copy(
            src_ref=coarse.at[r, t, c],
            dst_ref=coarse.at[r, t, c],
            send_sem=ag_send.at[r, k],
            recv_sem=ag_recv.at[r, k],
            device_id=((c + k) % clusters, t),
            device_id_type=MESH,
        )

    def ag_arrival(r, k):
        source = (c + clusters - k) % clusters
        return pltpu.make_async_remote_copy(
            src_ref=coarse.at[r, t, source],
            dst_ref=coarse.at[r, t, source],
            send_sem=ag_send.at[r, k],
            recv_sem=ag_recv.at[r, k],
            device_id=((c + k) % clusters, t),
            device_id_type=MESH,
        )

    def ag_start(r):
        @pl.loop(1, clusters)
        def _(k):
            ag_copy(r, k).start()

    def fwd_copy(r, which):
        return pltpu.make_async_remote_copy(
            src_ref=coarse.at[r, which],
            dst_ref=coarse.at[r, which],
            send_sem=fwd_send.at[r],
            recv_sem=fwd_recv.at[r],
            device_id=(c, other),
            device_id_type=MESH,
        )

    def ag_forward(r):
        @pl.loop(1, clusters)
        def _(k):
            ag_arrival(r, k).wait_recv()

        fwd_copy(r, t).start()

    def ag_finish(r):
        @pl.loop(1, clusters)
        def _(k):
            ag_copy(r, k).wait_send()

        fwd_copy(r, t).wait_send()
        fwd_copy(r, other).wait_recv()
        gathered = coarse[r].reshape(2 * clusters * 16, LANES)
        weights = jnp.dot(
            near[...].reshape(LANES, 2 * clusters * 16), gathered,
            precision=lax.Precision.HIGHEST, preferred_element_type=F32,
        )
        high = weights.astype(BF16)
        low = (weights - high.astype(F32)).astype(BF16)
        wide = jnp.concatenate(
            [jnp.concatenate([high, low], axis=1), jnp.concatenate([high, jnp.zeros_like(high)], axis=1)],
            axis=0,
        )
        return wide, jnp.sum(gathered.reshape(2 * clusters, 16, LANES), axis=0)

    start_all(halo_copies(modes_field, 0))
    start_all(near_groups())
    ag_start(0)

    @pl.loop(0, inner // TILE)
    def _(n):
        at = lax.broadcasted_iota(jnp.int32, (TILE, inner), 0) + n * TILE
        perm0[n] = (at == inner1[...]).astype(F32).astype(BF16)
        perm1[n] = (at == inner0[...]).astype(F32).astype(BF16)

    columns = jnp.transpose(outer[...])
    at = lax.broadcasted_iota(jnp.int32, (2 * ESUB, POOL), 1).astype(F32)
    total = jnp.zeros((2 * ESUB, POOL), F32)
    for n in range(3):
        total = total + (at == columns[:, n : n + 1]).astype(F32)
    share[...] = total.astype(BF16)

    def portion():
        return jnp.transpose(outer[...])[:, 3:4]

    @pl.loop(0, 2 * half)
    def _(chunk):
        buf = chunk % 2
        load(chunk, buf).wait()

        @pl.loop(0, BIG // 64)
        def _(n):
            at_rows = pl.ds(pl.multiple_of(n * 64, 64), 64)
            value = ops_buf[buf, at_rows, :]
            high = value.astype(BF16)
            ops_hi[chunk, at_rows, :] = high
            ops_lo[chunk, at_rows, :] = (value - high.astype(F32)).astype(BF16)

        @pl.when(chunk + 2 < 2 * half)
        def _():
            load(chunk + 2, buf).start()

    def tile_rows(n):
        return pl.ds(pl.multiple_of(n * TILE, TILE), TILE)

    def make_cat(source):
        @pl.loop(0, tiles)
        def _(n):
            cat[tile_rows(n), :] = split(source[n])

    def jump(source, r, groups, target):
        @pl.loop(0, inner // TILE)
        def _(n):
            picked = fold(mm(perm0[n], cat[rows + ESUB : 2 * rows, :]))
            target[1 + n] = 0.5 * (source[1 + n] - picked)
            back = fold(mm(perm1[n], cat[ESUB:rows, :]))
            target[per + 1 + n] = 0.5 * (source[per + 1 + n] - back)

        wait_all(groups)
        picked = fold(mm(share[...], split(pool[r])))
        scale = portion()
        target[0] = source[0] - (source[0] + picked[:ESUB]) * scale[:ESUB]
        target[per] = source[per] - (source[per] + picked[ESUB:]) * scale[ESUB:]

    def big_tile(n, emit):
        at_rows = pl.ds(pl.multiple_of((n // half) * rows, TILE), rows)
        out = fold(mm(ops_hi[n], cat[at_rows, :])) + mm(ops_lo[n], cat[at_rows, :LANES])
        emit(n, out)

    def store_image(n, out):
        image[2 * n] = out[:TILE]
        image[2 * n + 1] = out[TILE:]

    def store_image_cat(n, out):
        image_cat[pl.ds(pl.multiple_of(n * BIG, BIG), BIG), :] = split(out)

    def restrict():
        value = modes[...]
        high = value.astype(BF16)
        low = (value - high.astype(F32)).astype(BF16)
        out = mm(jnp.concatenate([high, low], axis=0), cat[...])
        return fold(out[:16]) + out[16:, :LANES]

    def put(r, terms, sums):
        row = lax.broadcasted_iota(jnp.int32, (16, LANES), 0)
        for n, value in enumerate(sums):
            terms = jnp.where(row == 12 + n, value, terms)
        coarse[r, t, c] = terms

    def row_sum(value):
        return jnp.sum(value, axis=0, keepdims=True)

    make_cat(modes_field)
    jump(modes_field, 0, halo_copies(modes_field, 0), field)

    @pl.loop(0, tiles)
    def _(n):
        value = split(field[n])
        lift_cat[tile_rows(n), :] = value
        cat[tile_rows(n), :] = value

    ag_forward(0)

    @pl.loop(0, 2 * half)
    def _(n):
        big_tile(n, store_image_cat)

    wait_all(near_groups())
    wide, _ = ag_finish(0)

    def start_tile(n):
        mult[n] = fold(mm(lift_cat[tile_rows(n), :], wide))
        value = rhs[n] - fold(mm(image_cat[tile_rows(n), :], wide))
        field[n] = value
        cat[tile_rows(n), :] = split(value)

    start_tile(0)
    start_tile(per)
    groups = halo_copies(field, 1)
    start_all(groups)

    @pl.loop(1, per)
    def _(n):
        start_tile(n)
        start_tile(per + n)

    jump(field, 1, groups, jumped)
    make_cat(jumped)
    put(1, restrict(), [])
    ag_start(1)

    @pl.loop(0, half)
    def _(n):
        big_tile(n, store_image)

    ag_forward(1)

    @pl.loop(half, 2 * half)
    def _(n):
        big_tile(n, store_image)

    wide, _ = ag_finish(1)

    def first_tile(n, carry):
        value = jumped[n] - fold(mm(lift_cat[tile_rows(n), :], wide))
        proj[n] = value
        made = image[n] - fold(mm(image_cat[tile_rows(n), :], wide))
        field[n] = made
        cat[tile_rows(n), :] = split(made)
        return carry[0] + row_sum(value * made), carry[1] + row_sum(value * value)

    zero = jnp.zeros((1, LANES), F32)
    carry = first_tile(per, first_tile(0, (zero, zero)))
    groups = halo_copies(field, 2)
    start_all(groups)
    carry = lax.fori_loop(1, per, lambda n, now: first_tile(per + n, first_tile(n, now)), carry)
    jump(field, 2, groups, jumped)
    make_cat(jumped)
    put(2, restrict(), carry)
    ag_start(2)

    @pl.loop(0, half)
    def _(n):
        big_tile(n, store_image)

    ag_forward(2)

    @pl.loop(half, 2 * half)
    def _(n):
        big_tile(n, store_image)

    wide, sums = ag_finish(2)
    curvature, norm = sums[12:13], sums[13:14]
    step = norm / curvature

    def second_tile(n, carry):
        moved = jumped[n] - fold(mm(lift_cat[tile_rows(n), :], wide))
        past[n] = moved
        old = proj[n]
        mult[n] = mult[n] + step * old
        new = old - step * moved
        old_made = field[n]
        made = old_made - step * (image[n] - fold(mm(image_cat[tile_rows(n), :], wide)))
        image[n] = made
        proj[n] = new
        jumped[n] = old
        cat[tile_rows(n), :] = split(made)
        return (
            carry[0] + row_sum(new * made),
            carry[1] + row_sum(new * old_made + old * made),
            carry[2] + row_sum(new * new),
        )

    carry = second_tile(per, second_tile(0, (zero, zero, zero)))
    groups = halo_copies(image, 3)
    start_all(groups)
    carry = lax.fori_loop(1, per, lambda n, now: second_tile(per + n, second_tile(n, now)), carry)
    jump(image, 3, groups, field)
    make_cat(field)
    put(3, restrict(), carry)
    ag_start(3)
    ag_forward(3)
    wide, sums = ag_finish(3)
    fresh, crossed, norm_next = sums[12:13], sums[13:14], sums[14:15]
    beta = norm_next / norm
    step_last = norm_next / (fresh + beta * (crossed + beta * curvature))

    @pl.loop(0, tiles)
    def _(n):
        moved = field[n] - fold(mm(lift_cat[tile_rows(n), :], wide))
        old = proj[n]
        mult[n] = mult[n] + step_last * (old + beta * jumped[n])
        proj[n] = old - step_last * (moved + beta * past[n])


def on_device(clusters, dual_ops, rigid_modes, members, coarse_inverse, dual_rhs, coarse_rhs):
    subs, rows, lanes = dual_rhs.shape
    modes_count = rigid_modes.shape[1]
    tiles = subs * rows // TILE
    local_rows = subs * rows
    export = subs * ESUB
    pad_index = local_rows + 6 * export
    inner = rows - ESUB
    c = lax.axis_index("clus")
    t = lax.axis_index("sub")
    slot = (c % 4) * 2 + t

    inner0 = (members[0, 1, ESUB:] - rows - ESUB)[None, :]
    inner1 = (members[1, 1, ESUB:] - ESUB)[None, :]

    names = jnp.transpose(members[:, :, :ESUB], (1, 0, 2)).reshape(-1, export)
    offset = names - local_rows
    block = offset // export
    within = offset % export
    cluster = block // 2
    own = (block % 2) == t
    sibling = jnp.where(within < 128, within, within - 256)
    lower = jnp.where(own, jnp.where(within < 256, within + 128, within), within + 256)
    upper = jnp.where(own, jnp.where(within < 384, within + 192, within + 128), within + 256)
    at = jnp.where(cluster == 0, lower, jnp.where(cluster == 1, sibling, upper))
    at = jnp.where(names < pad_index, at, -1).astype(F32)
    size = jnp.sum((names < pad_index).astype(F32), axis=0, keepdims=True)
    outer = jnp.concatenate([at[1:4], 1.0 / size, jnp.zeros((4, export), F32)], axis=0)

    count = subs * modes_count
    modes = jnp.concatenate(
        [
            jnp.pad(rigid_modes[0], ((0, 16 - modes_count), (0, rows))),
        ],
        axis=0,
    ) + jnp.pad(rigid_modes[1], ((modes_count, 16 - count), (rows, 0)))
    lane = lax.broadcasted_iota(jnp.int32, (8, 1, 1), 0)
    spread = jnp.where(lane == slot, modes[None], 0.0).reshape(LANES, local_rows)
    modes_field = jnp.transpose(spread).reshape(tiles, TILE, lanes)

    cinv = coarse_inverse.reshape(count, clusters, 2, count).transpose(0, 2, 1, 3)
    cinv = jnp.pad(cinv, ((0, 16 - count), (0, 0), (0, 0), (0, 16 - count)))
    cinv = cinv.reshape(16, 2 * clusters * 16)
    crhs = jnp.pad(coarse_rhs.reshape(count, lanes), ((0, 16 - count), (0, 0)))

    big = local_rows // BIG
    vmem = pl.BlockSpec(memory_space=pltpu.VMEM)
    shape = jax.ShapeDtypeStruct((tiles, TILE, lanes), F32)
    mult, proj = pl.pallas_call(
        functools.partial(kernel, clusters=clusters),
        out_shape=(shape, shape),
        in_specs=[pl.BlockSpec(memory_space=pl.ANY)] + [vmem] * 8,
        out_specs=(vmem, vmem),
        scratch_shapes=[
            pltpu.VMEM((big, BIG, rows), BF16),
            pltpu.VMEM((big, BIG, rows), BF16),
            pltpu.VMEM((2, BIG, rows), F32),
            pltpu.VMEM((inner // TILE, TILE, inner), BF16),
            pltpu.VMEM((inner // TILE, TILE, inner), BF16),
            pltpu.VMEM((export, POOL), BF16),
            pltpu.VMEM((local_rows, 2 * lanes), BF16),
            pltpu.VMEM((local_rows, 2 * lanes), BF16),
            pltpu.VMEM((local_rows, 2 * lanes), BF16),
            pltpu.VMEM((tiles, TILE, lanes), F32),
            pltpu.VMEM((tiles, TILE, lanes), F32),
            pltpu.VMEM((tiles, TILE, lanes), F32),
            pltpu.VMEM((tiles, TILE, lanes), F32),
            pltpu.VMEM((ROUNDS, POOL, lanes), F32),
            pltpu.VMEM((ROUNDS, 2, clusters, 16, lanes), F32),
            pltpu.VMEM((8, 16, 2 * clusters * 16), F32),
            pltpu.SemaphoreType.DMA((2,)),
            pltpu.SemaphoreType.DMA((ROUNDS, 8)),
            pltpu.SemaphoreType.DMA((ROUNDS, 8)),
            pltpu.SemaphoreType.DMA((5,)),
            pltpu.SemaphoreType.DMA((5,)),
            pltpu.SemaphoreType.DMA((ROUNDS, clusters)),
            pltpu.SemaphoreType.DMA((ROUNDS, clusters)),
            pltpu.SemaphoreType.DMA((ROUNDS,)),
            pltpu.SemaphoreType.DMA((ROUNDS,)),
        ],
        compiler_params=pltpu.CompilerParams(
            collective_id=0, has_side_effects=True, vmem_limit_bytes=60 * 2**20
        ),
    )(
        dual_ops.reshape(big, BIG, rows), modes_field, modes, inner0, inner1, outer, cinv,
        dual_rhs.reshape(tiles, TILE, lanes), crhs,
    )
    return mult.reshape(subs, rows, lanes), proj.reshape(subs, rows, lanes)


def solution(mesh):
    spec = P(("clus", "sub"), None, None)
    return jax.shard_map(
        functools.partial(on_device, mesh.shape["clus"]),
        mesh=mesh,
        in_specs=(spec, spec, spec, P(("clus", "sub"), None), spec, spec),
        out_specs=(spec, spec),
        check_vma=False,
    )
```

```python
import functools
import jax
import jax.numpy as jnp
from jax import lax
from jax.experimental import pallas as pl
from jax.experimental.pallas import tpu as pltpu
from jax.sharding import PartitionSpec as P

ESUB = 256
LANES = 128
TILE = 256
BIG = 512
POOL = 768
ROUNDS = 4
MESH = pl.DeviceIdType.MESH
F32 = jnp.float32
BF16 = jnp.bfloat16


def split(value):
    high = value.astype(BF16)
    low = (value - high.astype(F32)).astype(BF16)
    return jnp.concatenate([high, low], axis=1)


def mm(left, right):
    return jnp.dot(left, right, preferred_element_type=F32)


def fold(wide):
    return wide[:, :LANES] + wide[:, LANES:]


def kernel(
    ops_hbm, modes_in, members, cinv, rhs_hbm, crhs,
    mult, proj,
    ops_hi, ops_lo, ops_buf, perm0, perm1, share, lift_cat, image_cat, cat, cat2,
    field, jumped, image, past, pool, coarse, near, near_cat, modes, spread, outer, columns,
    ops_sem, rhs_sem, halo_send, halo_recv, near_send, near_recv, ag_send, ag_recv, fwd_send, fwd_recv,
    *, clusters,
):
    c = lax.axis_index("clus")
    t = lax.axis_index("sub")
    other = 1 - t
    has_up = c < clusters - 1
    has_down = c > 0
    up = jnp.minimum(c + 1, clusters - 1)
    down = jnp.maximum(c - 1, 0)
    slot = (c % 4) * 2 + t
    half = ops_hi.shape[0] // 2
    tiles = 2 * ops_hi.shape[0]
    per = tiles // 2
    rows = per * TILE
    inner = rows - ESUB

    def load(chunk, buf):
        return pltpu.make_async_copy(ops_hbm.at[chunk], ops_buf.at[buf], ops_sem.at[buf])

    def halo_copies(source, r):
        top, low = source.at[0], source.at[per]
        plan = [
            (top, 0, 128, 0, (c, other)),
            (low, 128, 128, 128, (c, other)),
            (top, 128, 128, 256, (up, t)),
            (low, 128, 64, 384, (up, t)),
            (low, 128, 64, 640, (up, other)),
            (low, 0, 128, 448, (down, t)),
            (low, 192, 64, 576, (down, t)),
            (low, 192, 64, 704, (down, other)),
        ]
        copies = [
            pltpu.make_async_remote_copy(
                src_ref=ref.at[pl.ds(start, size)],
                dst_ref=pool.at[r, pl.ds(to, size)],
                send_sem=halo_send.at[r, n],
                recv_sem=halo_recv.at[r, n],
                device_id=device,
                device_id_type=MESH,
            )
            for n, (ref, start, size, to, device) in enumerate(plan)
        ]
        return copies[:2], copies[2:5], copies[5:]

    def near_copies():
        return [
            pltpu.make_async_remote_copy(
                src_ref=cinv,
                dst_ref=near.at[slot],
                send_sem=near_send.at[n],
                recv_sem=near_recv.at[n],
                device_id=device,
                device_id_type=MESH,
            )
            for n, device in enumerate([(c, other), (up, t), (up, other), (down, t), (down, other)])
        ]

    def start_all(groups):
        both, ups, downs = groups

        @pl.when(has_up)
        def _():
            for copy in ups:
                copy.start()

        @pl.when(has_down)
        def _():
            for copy in downs:
                copy.start()

        for copy in both:
            copy.start()

    def wait_all(groups):
        both, ups, downs = groups
        for copy in both:
            copy.wait_recv()
            copy.wait_send()

        @pl.when(has_up)
        def _():
            for copy in ups:
                copy.wait_send()
            for copy in downs:
                copy.wait_recv()

        @pl.when(has_down)
        def _():
            for copy in downs:
                copy.wait_send()
            for copy in ups:
                copy.wait_recv()

    def near_groups():
        copies = near_copies()
        return copies[:1], copies[1:3], copies[3:]

    def ag_copy(r, k):
        return pltpu.make_async_remote_copy(
            src_ref=coarse.at[r, t, c],
            dst_ref=coarse.at[r, t, c],
            send_sem=ag_send.at[r, k],
            recv_sem=ag_recv.at[r, k],
            device_id=((c + k) % clusters, t),
            device_id_type=MESH,
        )

    def ag_arrival(r, k):
        source = (c + clusters - k) % clusters
        return pltpu.make_async_remote_copy(
            src_ref=coarse.at[r, t, source],
            dst_ref=coarse.at[r, t, source],
            send_sem=ag_send.at[r, k],
            recv_sem=ag_recv.at[r, k],
            device_id=((c + k) % clusters, t),
            device_id_type=MESH,
        )

    def ag_start(r):
        @pl.loop(1, clusters)
        def _(k):
            ag_copy(r, k).start()

    def fwd_copy(r, which):
        return pltpu.make_async_remote_copy(
            src_ref=coarse.at[r, which],
            dst_ref=coarse.at[r, which],
            send_sem=fwd_send.at[r],
            recv_sem=fwd_recv.at[r],
            device_id=(c, other),
            device_id_type=MESH,
        )

    def ag_forward(r):
        @pl.loop(1, clusters)
        def _(k):
            ag_arrival(r, k).wait_recv()

        fwd_copy(r, t).start()

    def ag_finish(r):
        @pl.loop(1, clusters)
        def _(k):
            ag_copy(r, k).wait_send()

        fwd_copy(r, t).wait_send()
        fwd_copy(r, other).wait_recv()
        gathered = coarse[r].reshape(2 * clusters * 16, LANES)
        out = mm(near_cat[...], split(gathered))
        weights = fold(out[:LANES]) + out[LANES:, :LANES]
        high = weights.astype(BF16)
        low = (weights - high.astype(F32)).astype(BF16)
        wide = jnp.concatenate(
            [jnp.concatenate([high, low], axis=1), jnp.concatenate([high, jnp.zeros_like(high)], axis=1)],
            axis=0,
        )
        return wide, jnp.sum(gathered.reshape(2 * clusters, 16, LANES), axis=0)

    load(0, 0).start()
    load(1, 1).start()

    near[...] = jnp.zeros_like(near)
    barrier = pltpu.get_barrier_semaphore()

    @pl.loop(1, clusters)
    def _(k):
        pl.semaphore_signal(barrier, inc=1, device_id=((c + k) % clusters, t), device_id_type=MESH)

    pl.semaphore_signal(barrier, inc=1, device_id=(c, other), device_id_type=MESH)

    @pl.when(has_up)
    def _():
        pl.semaphore_signal(barrier, inc=1, device_id=(up, other), device_id_type=MESH)

    @pl.when(has_down)
    def _():
        pl.semaphore_signal(barrier, inc=1, device_id=(down, other), device_id_type=MESH)

    rhs_copy = pltpu.make_async_copy(rhs_hbm, past, rhs_sem)
    rhs_copy.start()

    @pl.when(c == 0)
    def _():
        for r in range(ROUNDS):
            pool[r, 256:448, :] = jnp.zeros((192, LANES), F32)
            pool[r, 640:704, :] = jnp.zeros((64, LANES), F32)

    @pl.when(c == clusters - 1)
    def _():
        for r in range(ROUNDS):
            pool[r, 448:640, :] = jnp.zeros((192, LANES), F32)
            pool[r, 704:768, :] = jnp.zeros((64, LANES), F32)

    modes[...] = jnp.zeros_like(modes)
    for k in range(modes_in.shape[0]):
        modes[2 * k : 2 * k + 1, :rows] = modes_in[k, 0:1, :]
        modes[2 * k + 1 : 2 * k + 2, rows:] = modes_in[k, 1:2, :]
    spread[...] = jnp.zeros_like(spread)
    spread[pl.ds(pl.multiple_of(slot * 16, 16), 16), :] = modes[...]
    modes_field = image
    for n in (0, per):
        modes_field[n] = jnp.transpose(spread[:, n * TILE : (n + 1) * TILE])

    coarse[0, t, c] = jnp.zeros((16, LANES), F32)
    for k in range(crhs.shape[0]):
        coarse[0, t, c, 2 * k : 2 * k + 2, :] = crhs[k]
    near[slot] = cinv[...]

    @pl.loop(0, inner // TILE)
    def _(n):
        at = lax.broadcasted_iota(jnp.int32, (TILE, inner), 0) + n * TILE
        perm0[n] = (at == members[1, 1:2, ESUB:] - ESUB).astype(F32).astype(BF16)
        perm1[n] = (at == members[0, 1:2, ESUB:] - (rows + ESUB)).astype(F32).astype(BF16)

    names = jnp.concatenate([members[0, :, :ESUB], members[1, :, :ESUB]], axis=1)
    offset = names - 2 * rows
    block = lax.shift_right_arithmetic(offset, 9)
    within = offset & (2 * ESUB - 1)
    cluster = lax.shift_right_arithmetic(block, 1)
    own = (block & 1) == t
    sibling = jnp.where(within < 128, within, within - 256)
    lower = jnp.where(own, jnp.where(within < 256, within + 128, within), within + 256)
    upper = jnp.where(own, jnp.where(within < 384, within + 192, within + 128), within + 256)
    place = jnp.where(cluster == 0, lower, jnp.where(cluster == 1, sibling, upper))
    named = names < 2 * rows + 12 * ESUB
    place = jnp.where(named, place, -1).astype(F32)
    size = jnp.sum(named.astype(F32), axis=0, keepdims=True)
    row = lax.broadcasted_iota(jnp.int32, place.shape, 0)
    outer[...] = jnp.zeros_like(outer)
    outer[0:4, :] = jnp.where(row == 0, 1.0 / size, place)
    columns[...] = jnp.transpose(outer[...])
    at = lax.broadcasted_iota(jnp.int32, (2 * ESUB, POOL), 1).astype(F32)
    total = jnp.zeros((2 * ESUB, POOL), F32)
    for n in range(1, 4):
        total = total + (at == columns[:, n : n + 1]).astype(F32)
    share[...] = total.astype(BF16)

    @pl.when(has_up & has_down)
    def _():
        pl.semaphore_wait(barrier, clusters + 2)

    @pl.when(jnp.logical_not(has_up & has_down))
    def _():
        pl.semaphore_wait(barrier, clusters + 1)

    start_all(halo_copies(modes_field, 0))
    start_all(near_groups())
    ag_start(0)

    for n in range(tiles):
        if n % per:
            modes_field[n] = jnp.transpose(spread[:, n * TILE : (n + 1) * TILE])

    @pl.loop(0, 2 * half)
    def _(chunk):
        buf = chunk % 2
        load(chunk, buf).wait()

        @pl.loop(0, BIG // 64)
        def _(n):
            at_rows = pl.ds(pl.multiple_of(n * 64, 64), 64)
            value = ops_buf[buf, at_rows, :]
            high = value.astype(BF16)
            ops_hi[chunk, at_rows, :] = high
            ops_lo[chunk, at_rows, :] = (value - high.astype(F32)).astype(BF16)

        @pl.when(chunk + 2 < 2 * half)
        def _():
            load(chunk + 2, buf).start()

    def tile_rows(n):
        return pl.ds(n * TILE, TILE)

    def jump(source, r, groups, target, target_cat):
        def emit(n, value):
            target[n] = value
            target_cat[n * TILE : (n + 1) * TILE, :] = split(value)

        for n in range(inner // TILE):
            picked = fold(mm(perm0[n], cat[rows + ESUB : 2 * rows, :]))
            emit(1 + n, 0.5 * (source[1 + n] - picked))
            back = fold(mm(perm1[n], cat[ESUB:rows, :]))
            emit(per + 1 + n, 0.5 * (source[per + 1 + n] - back))

        wait_all(groups)
        picked = fold(mm(share[...], split(pool[r])))
        scale = columns[:, 0:1]
        emit(0, source[0] - (source[0] + picked[:ESUB]) * scale[:ESUB])
        emit(per, source[per] - (source[per] + picked[ESUB:]) * scale[ESUB:])

    def big_tile(n, emit, cat):
        at_rows = pl.ds(pl.multiple_of((n // half) * rows, TILE), rows)
        out = fold(mm(ops_hi[n], cat[at_rows, :])) + mm(ops_lo[n], cat[at_rows, :LANES])
        emit(n, out)

    def store_image(n, out):
        image[2 * n] = out[:TILE]
        image[2 * n + 1] = out[TILE:]

    def store_image_cat(n, out):
        image_cat[pl.ds(pl.multiple_of(n * BIG, BIG), BIG), :] = split(out)

    def restrict():
        value = modes[...]
        high = value.astype(BF16)
        low = (value - high.astype(F32)).astype(BF16)
        out = mm(jnp.concatenate([high, low], axis=0), cat2[...])
        return fold(out[:16]) + out[16:, :LANES]

    def put(r, terms, sums):
        row = lax.broadcasted_iota(jnp.int32, (16, LANES), 0)
        for n, value in enumerate(sums):
            terms = jnp.where(row == 12 + n, value, terms)
        coarse[r, t, c] = terms

    def row_sum(value):
        return jnp.sum(value, axis=0, keepdims=True)

    for n in range(tiles):
        cat[n * TILE : (n + 1) * TILE, :] = split(modes_field[n])
    jump(modes_field, 0, halo_copies(modes_field, 0), field, lift_cat)

    ag_forward(0)

    @pl.loop(0, 2 * half)
    def _(n):
        big_tile(n, store_image_cat, lift_cat)

    wait_all(near_groups())
    whole = near[...].reshape(LANES, 2 * clusters * 16)
    whole_high = whole.astype(BF16)
    near_cat[:LANES, :] = whole_high
    near_cat[LANES:, :] = (whole - whole_high.astype(F32)).astype(BF16)
    wide, _ = ag_finish(0)

    def start_tile(n):
        mult[n] = fold(mm(lift_cat[tile_rows(n), :], wide))
        value = past[n] - fold(mm(image_cat[tile_rows(n), :], wide))
        field[n] = value
        cat[tile_rows(n), :] = split(value)

    rhs_copy.wait()
    start_tile(0)
    start_tile(per)
    groups = halo_copies(field, 1)
    start_all(groups)

    for n in range(1, per):
        start_tile(n)
        start_tile(per + n)

    jump(field, 1, groups, jumped, cat2)
    put(1, restrict(), [])
    ag_start(1)

    @pl.loop(0, half)
    def _(n):
        big_tile(n, store_image, cat2)

    ag_forward(1)

    @pl.loop(half, 2 * half)
    def _(n):
        big_tile(n, store_image, cat2)

    wide, _ = ag_finish(1)

    def first_tile(n, carry):
        value = jumped[n] - fold(mm(lift_cat[tile_rows(n), :], wide))
        proj[n] = value
        made = image[n] - fold(mm(image_cat[tile_rows(n), :], wide))
        field[n] = made
        cat[tile_rows(n), :] = split(made)
        return carry[0] + row_sum(value * made), carry[1] + row_sum(value * value)

    zero = jnp.zeros((1, LANES), F32)
    carry = first_tile(per, first_tile(0, (zero, zero)))
    groups = halo_copies(field, 2)
    start_all(groups)
    for n in range(1, per):
        carry = first_tile(per + n, first_tile(n, carry))
    jump(field, 2, groups, jumped, cat2)
    put(2, restrict(), carry)
    ag_start(2)

    @pl.loop(0, half)
    def _(n):
        big_tile(n, store_image, cat2)

    ag_forward(2)

    @pl.loop(half, 2 * half)
    def _(n):
        big_tile(n, store_image, cat2)

    wide, sums = ag_finish(2)
    curvature, norm = sums[12:13], sums[13:14]
    step = norm / curvature

    def second_tile(n, carry):
        moved = jumped[n] - fold(mm(lift_cat[tile_rows(n), :], wide))
        past[n] = moved
        old = proj[n]
        mult[n] = mult[n] + step * old
        new = old - step * moved
        old_made = field[n]
        made = old_made - step * (image[n] - fold(mm(image_cat[tile_rows(n), :], wide)))
        image[n] = made
        proj[n] = new
        jumped[n] = old
        cat[tile_rows(n), :] = split(made)
        return (
            carry[0] + row_sum(new * made),
            carry[1] + row_sum(new * old_made + old * made),
            carry[2] + row_sum(new * new),
        )

    carry = second_tile(per, second_tile(0, (zero, zero, zero)))
    groups = halo_copies(image, 3)
    start_all(groups)
    for n in range(1, per):
        carry = second_tile(per + n, second_tile(n, carry))
    jump(image, 3, groups, field, cat2)
    put(3, restrict(), carry)
    ag_start(3)
    ag_forward(3)
    wide, sums = ag_finish(3)
    fresh, crossed, norm_next = sums[12:13], sums[13:14], sums[14:15]
    beta = norm_next / norm
    step_last = norm_next / (fresh + beta * (crossed + beta * curvature))

    for n in range(tiles):
        moved = field[n] - fold(mm(lift_cat[tile_rows(n), :], wide))
        old = proj[n]
        mult[n] = mult[n] + step_last * (old + beta * jumped[n])
        proj[n] = old - step_last * (moved + beta * past[n])


def on_device(clusters, dual_ops, rigid_modes, members, coarse_inverse, dual_rhs, coarse_rhs):
    subs, rows, lanes = dual_rhs.shape
    modes_count = rigid_modes.shape[1]
    tiles = subs * rows // TILE
    local_rows = subs * rows
    export = subs * ESUB
    inner = rows - ESUB

    count = subs * modes_count
    cinv = coarse_inverse.reshape(subs, modes_count, clusters, 2, subs, modes_count)
    cinv = cinv.transpose(1, 0, 3, 2, 5, 4).reshape(count, 2, clusters, count)
    cinv = jnp.pad(cinv, ((0, 16 - count), (0, 0), (0, 0), (0, 16 - count)))
    cinv = cinv.reshape(16, 2 * clusters * 16)

    big = local_rows // BIG
    vmem = pl.BlockSpec(memory_space=pltpu.VMEM)
    hbm = pl.BlockSpec(memory_space=pl.ANY)
    shape = jax.ShapeDtypeStruct((tiles, TILE, lanes), F32)
    mult, proj = pl.pallas_call(
        functools.partial(kernel, clusters=clusters),
        out_shape=(shape, shape),
        in_specs=[hbm, vmem, vmem, vmem, hbm, vmem],
        out_specs=(vmem, vmem),
        scratch_shapes=[
            pltpu.VMEM((big, BIG, rows), BF16),
            pltpu.VMEM((big, BIG, rows), BF16),
            pltpu.VMEM((2, BIG, rows), F32),
            pltpu.VMEM((inner // TILE, TILE, inner), BF16),
            pltpu.VMEM((inner // TILE, TILE, inner), BF16),
            pltpu.VMEM((export, POOL), BF16),
            pltpu.VMEM((local_rows, 2 * lanes), BF16),
            pltpu.VMEM((local_rows, 2 * lanes), BF16),
            pltpu.VMEM((local_rows, 2 * lanes), BF16),
            pltpu.VMEM((local_rows, 2 * lanes), BF16),
            pltpu.VMEM((tiles, TILE, lanes), F32),
            pltpu.VMEM((tiles, TILE, lanes), F32),
            pltpu.VMEM((tiles, TILE, lanes), F32),
            pltpu.VMEM((tiles, TILE, lanes), F32),
            pltpu.VMEM((ROUNDS, POOL, lanes), F32),
            pltpu.VMEM((ROUNDS, 2, clusters, 16, lanes), F32),
            pltpu.VMEM((8, 16, 2 * clusters * 16), F32),
            pltpu.VMEM((2 * LANES, 2 * clusters * 16), BF16),
            pltpu.VMEM((16, local_rows), F32),
            pltpu.VMEM((LANES, local_rows), F32),
            pltpu.VMEM((8, export), F32),
            pltpu.VMEM((export, 8), F32),
            pltpu.SemaphoreType.DMA((2,)),
            pltpu.SemaphoreType.DMA,
            pltpu.SemaphoreType.DMA((ROUNDS, 8)),
            pltpu.SemaphoreType.DMA((ROUNDS, 8)),
            pltpu.SemaphoreType.DMA((5,)),
            pltpu.SemaphoreType.DMA((5,)),
            pltpu.SemaphoreType.DMA((ROUNDS, clusters)),
            pltpu.SemaphoreType.DMA((ROUNDS, clusters)),
            pltpu.SemaphoreType.DMA((ROUNDS,)),
            pltpu.SemaphoreType.DMA((ROUNDS,)),
        ],
        compiler_params=pltpu.CompilerParams(
            collective_id=0, has_side_effects=True, vmem_limit_bytes=60 * 2**20
        ),
    )(
        dual_ops.reshape(big, BIG, rows), jnp.transpose(rigid_modes, (1, 0, 2)), members, cinv,
        dual_rhs.reshape(tiles, TILE, lanes), jnp.transpose(coarse_rhs, (1, 0, 2)),
    )
    return mult.reshape(subs, rows, lanes), proj.reshape(subs, rows, lanes)


def solution(mesh):
    spec = P(("clus", "sub"), None, None)
    return jax.shard_map(
        functools.partial(on_device, mesh.shape["clus"]),
        mesh=mesh,
        in_specs=(spec, spec, spec, P(("clus", "sub"), None), spec, spec),
        out_specs=(spec, spec),
        check_vma=False,
    )
```
